32 devices in a mesh: clip: 2 (over x), seq: 16 (over z, y, core).
Axes of the slice: x: 2, y: 2, z: 4, core: 2. Of those that a mesh axis runs over, the one named last changes fastest.
Arguments:
- video_query: bfloat16 [512, 4096], P(('clip', 'seq')), parts along dimension 0, may hold values from -6 to 6
- video_keys: bfloat16 [512, 4096], P(('clip', 'seq')), parts along dimension 0, may hold values from -6 to 6
- video_values: bfloat16 [512, 4096], P(('clip', 'seq')), parts along dimension 0, may hold values from -6 to 6
- audio_query: bfloat16 [256, 2048], P(('clip', 'seq')), parts along dimension 0, may hold values from -6 to 6
- audio_keys: bfloat16 [256, 2048], P(('clip', 'seq')), parts along dimension 0, may hold values from -6 to 6
- audio_values: bfloat16 [256, 2048], P(('clip', 'seq')), parts along dimension 0, may hold values from -6 to 6
- cross_video_query: bfloat16 [512, 2048], P(('clip', 'seq')), parts along dimension 0, may hold values from -6 to 6
- cross_video_keys: bfloat16 [512, 2048], P(('clip', 'seq')), parts along dimension 0, may hold values from -6 to 6
- cross_video_values: bfloat16 [512, 2048], P(('clip', 'seq')), parts along dimension 0, may hold values from -6 to 6
- cross_audio_query: bfloat16 [256, 2048], P(('clip', 'seq')), parts along dimension 0, may hold values from -6 to 6
- cross_audio_keys: bfloat16 [256, 2048], P(('clip', 'seq')), parts along dimension 0, may hold values from -6 to 6
- cross_audio_values: bfloat16 [256, 2048], P(('clip', 'seq')), parts along dimension 0, may hold values from -6 to 6
- video_length: int32 [2], P('clip'), parts along dimension 0, may hold values from 128 to 256
- audio_length: int32 [2], P('clip'), parts along dimension 0, may hold values from 64 to 128
- align_offset: int32 [2], P('clip'), parts along dimension 0, may hold values from -8 to 8
Outputs:
- video_mixed: bfloat16 [512, 4096], P(('clip', 'seq')), parts along dimension 0
- audio_mixed: bfloat16 [256, 2048], P(('clip', 'seq')), parts along dimension 0
- video_cross: bfloat16 [512, 2048], P(('clip', 'seq')), parts along dimension 0
- audio_cross: bfloat16 [256, 2048], P(('clip', 'seq')), parts along dimension 0
The draws below stay inside these ranges and needn't reach their ends.
There are 2 independent parts, one for each index of `clip`. The reference program is written for one: setup_inputs(seed, part) draws one part's arguments, and reference() takes and returns one part's arrays. A program takes and returns all parts, laid end to end along the dimension named above; each array names one. Nothing has to cross between parts.
All inputs are finite; a program needn't handle non-finite values.
Results may differ from the reference program's by a relative error of at most 0.006.
Values may be sent and summed in bfloat16 or wider, within the bound.
A program may use at most 128 MiB of HBM per device.

```python
import math
import jax
import jax.numpy as jnp
from jax import lax

HV = 32
HDV = 128
HA = 32
HDA = 64
DV = 4096
DA = 2048
TV = 256
TA = 128
AWIN = 80
VWIN = 32


def base_field(key, rows, width):
    values = jnp.clip(jax.random.normal(key, (rows, width), dtype=jnp.float32), -6.0, 6.0)
    return values


def plant_queries(values, key):
    return values.astype(jnp.bfloat16)


def plant_keys(values, key):
    return values.astype(jnp.bfloat16)


def draw_video_query(key, part):
    return plant_queries(base_field(jax.random.fold_in(key, 101), TV, DV), key)


def draw_video_keys(key, part):
    return plant_keys(base_field(jax.random.fold_in(key, 102), TV, DV), key)


def draw_audio_query(key, part):
    return plant_queries(base_field(jax.random.fold_in(key, 103), TA, DA), key)


def draw_audio_keys(key, part):
    return plant_keys(base_field(jax.random.fold_in(key, 104), TA, DA), key)


def draw_cross_video_query(key, part):
    return plant_queries(base_field(jax.random.fold_in(key, 105), TV, DA), key)


def draw_cross_audio_keys(key, part):
    return plant_keys(base_field(jax.random.fold_in(key, 106), TA, DA), key)


def draw_cross_audio_query(key, part):
    return plant_queries(base_field(jax.random.fold_in(key, 107), TA, DA), key)


def draw_cross_video_keys(key, part):
    return plant_keys(base_field(jax.random.fold_in(key, 108), TV, DA), key)


def level_of(key, extent, pieces, least, largest):
    def one(axis_at, parts):
        heights = jax.random.uniform(jax.random.fold_in(jax.random.fold_in(key, 6), axis_at), (parts,), jnp.float32, least / len(pieces), largest / len(pieces))
        return jnp.repeat(jnp.exp(heights), extent[axis_at] // parts).reshape((-1,) + (1,) * (len(extent) - axis_at - 1))

    factor_of = one(*pieces[0])
    for cut in pieces[1:]:
        factor_of = factor_of * one(*cut)
    return factor_of


def gaussian(rng, shape, scale, reach, shards=(), kind=jnp.bfloat16):
    level = level_of(rng, shape, shards, -0.22, 0.18) if shards else 1.0
    values = jax.random.normal(rng, shape, jnp.float32) * scale * level
    return jnp.minimum(jnp.maximum(values, -reach), reach).astype(kind)


def setup_inputs(seed: int = 0, part: int = 0) -> dict:
    splits = jax.random.split(jax.random.key(seed), 16)
    part_splits = jax.random.split(jax.random.fold_in(splits[15], part), 16)
    return {
        "video_query": draw_video_query(jax.random.fold_in(jax.random.fold_in(splits[15], part), 71), part),
        "video_keys": draw_video_keys(jax.random.fold_in(jax.random.fold_in(splits[15], part), 71), part),
        "video_values": gaussian(part_splits[2], (TV, DV), 1.0, 6.0, ((0, 16),)),
        "audio_query": draw_audio_query(jax.random.fold_in(jax.random.fold_in(splits[15], part), 71), part),
        "audio_keys": draw_audio_keys(jax.random.fold_in(jax.random.fold_in(splits[15], part), 71), part),
        "audio_values": gaussian(part_splits[5], (TA, DA), 1.0, 6.0, ((0, 16),)),
        "cross_video_query": draw_cross_video_query(jax.random.fold_in(jax.random.fold_in(splits[15], part), 71), part),
        "cross_video_keys": draw_cross_video_keys(jax.random.fold_in(jax.random.fold_in(splits[15], part), 71), part),
        "cross_video_values": gaussian(part_splits[8], (TV, DA), 1.0, 6.0, ((0, 16),)),
        "cross_audio_query": draw_cross_audio_query(jax.random.fold_in(jax.random.fold_in(splits[15], part), 71), part),
        "cross_audio_keys": draw_cross_audio_keys(jax.random.fold_in(jax.random.fold_in(splits[15], part), 71), part),
        "cross_audio_values": gaussian(part_splits[11], (TA, DA), 1.0, 6.0, ((0, 16),)),
        "video_length": jax.random.randint(part_splits[12], (1,), TV // 2, TV + 1).astype(jnp.int32),
        "audio_length": jax.random.randint(part_splits[13], (1,), TA // 2, TA + 1).astype(jnp.int32),
        "align_offset": jax.random.randint(part_splits[14], (1,), -(TA // 16), TA // 16 + 1).astype(jnp.int32),
    }


def block_size(total, limit):
    chosen = min(total, limit)
    while total % chosen:
        chosen -= 1
    return chosen

def exact_attention(queries, keys, values, heads, depth, query_pos, key_pos, allowed):
    count = queries.shape[0]
    key_count = keys.shape[0]
    head_queries = queries.reshape(count, heads, depth).transpose(1, 0, 2)
    head_keys = keys.reshape(key_count, heads, depth).transpose(1, 0, 2)
    head_values = values.reshape(key_count, heads, depth).transpose(1, 0, 2)
    q_block = block_size(count, 512)
    scale = 1.0 / math.sqrt(depth)
    places = query_pos.reshape(count // q_block, q_block)

    def one_head(packed):
        one_query, one_key, one_value = packed
        tiles = one_query.reshape(count // q_block, q_block, depth)

        def one_tile(tile_pack):
            tile, tile_pos = tile_pack
            scores = jnp.dot(tile, one_key.T, preferred_element_type=jnp.float32) * scale
            permit = allowed(tile_pos[:, None], key_pos[None, :])
            scores = jnp.where(permit, scores, -jnp.inf)
            peak = lax.optimization_barrier(jnp.max(scores, axis=1, keepdims=True))
            weights = jnp.exp(scores - peak)
            total = lax.optimization_barrier(jnp.sum(weights, axis=1, keepdims=True))
            mixed = jnp.dot(weights.astype(jnp.bfloat16), one_value, preferred_element_type=jnp.float32)
            return (mixed / total).astype(jnp.bfloat16)
        return lax.map(one_tile, (tiles, places)).reshape(count, depth)
    result = lax.map(one_head, (head_queries, head_keys, head_values))
    return result.transpose(1, 0, 2).reshape(count, heads * depth)

def reference(video_query, video_keys, video_values, audio_query, audio_keys, audio_values, cross_video_query, cross_video_keys, cross_video_values, cross_audio_query, cross_audio_keys, cross_audio_values, video_length, audio_length, align_offset):
    video_valid = video_length[0]
    audio_valid = audio_length[0]
    align_shift = align_offset[0]
    video_places = jnp.arange(TV, dtype=jnp.int32)
    audio_places = jnp.arange(TA, dtype=jnp.int32)

    def video_open(q_where, k_where):
        return k_where < video_valid

    def audio_open(q_where, k_where):
        return k_where < audio_valid

    def toward_video(q_where, k_where):
        center = jnp.clip(q_where * TA // TV + align_shift, 0, audio_valid - 1)
        return (k_where < audio_valid) & (jnp.abs(k_where - center) <= AWIN)

    def toward_audio(q_where, k_where):
        center = jnp.clip((q_where - align_shift) * TV // TA, 0, video_valid - 1)
        return (k_where < video_valid) & (jnp.abs(k_where - center) <= VWIN)
    video_mixed = exact_attention(video_query, video_keys, video_values, HV, HDV, video_places, video_places, video_open)
    audio_mixed = exact_attention(audio_query, audio_keys, audio_values, HA, HDA, audio_places, audio_places, audio_open)
    video_cross = exact_attention(cross_video_query, cross_audio_keys, cross_audio_values, HA, HDA, video_places, audio_places, toward_video)
    audio_cross = exact_attention(cross_audio_query, cross_video_keys, cross_video_values, HA, HDA, audio_places, video_places, toward_audio)
    return (video_mixed, audio_mixed, video_cross, audio_cross)
```

```python
import functools
import math

import jax
import jax.numpy as jnp
from jax import lax
from jax.experimental import pallas as pl
from jax.experimental.pallas import tpu as pltpu
from jax.sharding import PartitionSpec as P

HV = 32
HDV = 128
HA = 32
HDA = 64


def block_size(total, limit):
    chosen = min(total, limit)
    while total % chosen:
        chosen -= 1
    return chosen


def split_heads(tokens, heads, depth, copies):
    rows = tokens.shape[0]
    shaped = tokens.reshape(copies, rows // copies, heads, depth).transpose(2, 0, 1, 3)
    return shaped.reshape(heads * copies, rows // copies, depth)


def spread_heads(tokens, heads, depth, copies):
    rows = tokens.shape[0]
    shaped = tokens.reshape(rows, heads, depth).transpose(1, 0, 2)
    shaped = jnp.broadcast_to(shaped[:, None], (heads, copies, rows, depth))
    return shaped.reshape(heads * copies, rows, depth)


def join_heads(owned, heads, depth, copies):
    part_rows = owned.shape[1]
    shaped = owned.reshape(heads, copies, part_rows, depth).transpose(1, 2, 0, 3)
    return shaped.reshape(copies * part_rows, heads * depth)


def owned_positions(rows, copies, devices, index):
    part_rows = rows // copies
    flat = jnp.arange(devices * part_rows, dtype=jnp.int32)
    return flat // part_rows * rows + index % copies * part_rows + flat % part_rows


def online_update(carry, scores, permit, value_tile, value_form):
    running, total, accum = carry
    scores = jnp.where(permit, scores, -1e30)
    newmax = jnp.maximum(running, jnp.max(scores, axis=2))
    weights = jnp.where(permit, jnp.exp(scores - newmax[:, :, None]), 0.0)
    factor = jnp.exp(running - newmax)
    total = total * factor + jnp.sum(weights, axis=2)
    mixed = jnp.einsum(
        value_form, weights.astype(jnp.bfloat16), value_tile, preferred_element_type=jnp.float32
    )
    accum = accum * factor[:, :, None] + mixed
    return (newmax, total, accum)


def fold_initial(rows, heads, depth):
    return (
        jnp.full((heads, rows), -1e30, jnp.float32),
        jnp.zeros((heads, rows), jnp.float32),
        jnp.zeros((heads, rows, depth), jnp.float32),
    )


def fold_piece(carry, local_query, key_rows, value_rows, permit, heads, depth):
    keyed = key_rows.reshape(key_rows.shape[0], heads, depth)
    valued = value_rows.reshape(value_rows.shape[0], heads, depth)
    scores = jnp.einsum("qhd,khd->hqk", local_query, keyed, preferred_element_type=jnp.float32) * (
        1.0 / math.sqrt(depth)
    )
    return online_update(carry, scores, permit[None], valued, "hqk,khd->hqd")


def fold_finish(carry, heads, depth):
    running, total, accum = carry
    result = (accum / total[:, :, None]).astype(jnp.bfloat16)
    return result.transpose(1, 0, 2).reshape(result.shape[1], heads * depth)


def attend_local(queries, keys, values, query_pos, key_pos, allowed):
    heads, q_count, depth = queries.shape
    k_count = keys.shape[1]
    q_block = block_size(q_count, 512)
    k_block = block_size(k_count, 2048)
    scale = 1.0 / math.sqrt(depth)
    q_tiles = queries.reshape(heads, q_count // q_block, q_block, depth).transpose(1, 0, 2, 3)
    k_tiles = keys.reshape(heads, k_count // k_block, k_block, depth).transpose(1, 0, 2, 3)
    v_tiles = values.reshape(heads, k_count // k_block, k_block, depth).transpose(1, 0, 2, 3)
    q_places = query_pos.reshape(q_count // q_block, q_block)
    k_places = key_pos.reshape(k_count // k_block, k_block)

    def one_tile(packed):
        q_tile, q_where = packed

        def absorb(carry, piece):
            k_tile, v_tile, k_where = piece
            scores = (
                jnp.einsum("hqd,hkd->hqk", q_tile, k_tile, preferred_element_type=jnp.float32)
                * scale
            )
            permit = allowed(q_where[:, None], k_where[None, :])[None]
            return (online_update(carry, scores, permit, v_tile, "hqk,hkd->hqd"), None)

        initial = fold_initial(q_block, heads, depth)
        final_state, unused = lax.scan(absorb, initial, (k_tiles, v_tiles, k_places))
        running, total, accum = final_state
        return (accum / total[:, :, None]).astype(jnp.bfloat16)

    tiles = lax.map(one_tile, (q_tiles, q_places))
    return tiles.transpose(1, 0, 2, 3).reshape(heads, q_count, depth)


def shards(
    video_query,
    video_keys,
    video_values,
    audio_query,
    audio_keys,
    audio_values,
    cross_video_query,
    cross_video_keys,
    cross_video_values,
    cross_audio_query,
    cross_audio_keys,
    cross_audio_values,
    video_length,
    audio_length,
    align_offset,
):
    devices = lax.axis_size("seq")
    index = lax.axis_index("seq")
    video_rows = video_query.shape[0]
    audio_rows = audio_query.shape[0]
    video_total = video_rows * devices
    audio_total = audio_rows * devices
    video_reach = video_total // 8
    audio_reach = 5 * audio_total // 8
    video_valid = video_length[0]
    audio_valid = audio_length[0]
    align_shift = align_offset[0]
    copies = max(devices // HV, 1)
    video_places = jnp.arange(video_total, dtype=jnp.int32)
    audio_places = jnp.arange(audio_total, dtype=jnp.int32)

    def video_open(q_where, k_where):
        return k_where < video_valid

    def toward_video(q_where, k_where):
        center = jnp.clip(q_where * audio_total // video_total + align_shift, 0, audio_valid - 1)
        return (k_where < audio_valid) & (jnp.abs(k_where - center) <= audio_reach)

    def toward_audio(q_where, k_where):
        center = jnp.clip((q_where - align_shift) * video_total // audio_total, 0, video_valid - 1)
        return (k_where < video_valid) & (jnp.abs(k_where - center) <= video_reach)

    video_owned = (
        lax.all_to_all(
            split_heads(video_query, HV, HDV, copies),
            "seq",
            split_axis=0,
            concat_axis=1,
            tiled=True,
        ),
        lax.all_to_all(
            spread_heads(video_keys, HV, HDV, copies),
            "seq",
            split_axis=0,
            concat_axis=1,
            tiled=True,
        ),
        lax.all_to_all(
            spread_heads(video_values, HV, HDV, copies),
            "seq",
            split_axis=0,
            concat_axis=1,
            tiled=True,
        ),
    )
    video_done = attend_local(
        video_owned[0],
        video_owned[1],
        video_owned[2],
        owned_positions(video_rows, copies, devices, index),
        video_places,
        video_open,
    )
    video_mixed = join_heads(
        lax.all_to_all(video_done, "seq", split_axis=1, concat_axis=0, tiled=True), HV, HDV, copies
    )
    audio_local = audio_query.reshape(audio_rows, HA, HDA)
    piece = (
        lax.all_gather(audio_keys, "seq", axis=0, tiled=True),
        lax.all_gather(audio_values, "seq", axis=0, tiled=True),
    )
    k_where = jnp.arange(piece[0].shape[0], dtype=jnp.int32)
    audio_k_where = k_where[None, :]
    permit = audio_k_where < audio_valid
    audio_state = fold_piece(
        fold_initial(audio_rows, HA, HDA), audio_local, piece[0], piece[1], permit, HA, HDA
    )
    audio_mixed = fold_finish(audio_state, HA, HDA)
    cross_owned = (
        lax.all_to_all(
            split_heads(cross_video_query, HA, HDA, copies),
            "seq",
            split_axis=0,
            concat_axis=1,
            tiled=True,
        ),
        lax.all_to_all(
            spread_heads(cross_audio_keys, HA, HDA, copies),
            "seq",
            split_axis=0,
            concat_axis=1,
            tiled=True,
        ),
        lax.all_to_all(
            spread_heads(cross_audio_values, HA, HDA, copies),
            "seq",
            split_axis=0,
            concat_axis=1,
            tiled=True,
        ),
    )
    cross_done = attend_local(
        cross_owned[0],
        cross_owned[1],
        cross_owned[2],
        owned_positions(video_rows, copies, devices, index),
        audio_places,
        toward_video,
    )
    video_cross = join_heads(
        lax.all_to_all(cross_done, "seq", split_axis=1, concat_axis=0, tiled=True), HA, HDA, copies
    )
    listen_owned = (
        lax.all_to_all(
            split_heads(cross_audio_query, HA, HDA, copies),
            "seq",
            split_axis=0,
            concat_axis=1,
            tiled=True,
        ),
        lax.all_to_all(
            spread_heads(cross_video_keys, HA, HDA, copies),
            "seq",
            split_axis=0,
            concat_axis=1,
            tiled=True,
        ),
        lax.all_to_all(
            spread_heads(cross_video_values, HA, HDA, copies),
            "seq",
            split_axis=0,
            concat_axis=1,
            tiled=True,
        ),
    )
    listen_done = attend_local(
        listen_owned[0],
        listen_owned[1],
        listen_owned[2],
        owned_positions(audio_rows, copies, devices, index),
        video_places,
        toward_audio,
    )
    audio_cross = join_heads(
        lax.all_to_all(listen_done, "seq", split_axis=1, concat_axis=0, tiled=True), HA, HDA, copies
    )
    return (video_mixed, audio_mixed, video_cross, audio_cross)


LANES = 128

GROUPS = ((0, 1, 2), (6, 10, 11), (9, 7, 8), (3, 4, 5))
OUT_OF_GROUP = (0, 2, 3, 1)


def softmax_mix(query, keys, values, permit, scale):
    scores = lax.dot_general(
        query, keys, (((1,), (1,)), ((), ())), preferred_element_type=jnp.float32
    )
    scores = jnp.where(permit, scores * scale, -1e30)
    peak = jnp.max(scores, axis=1, keepdims=True)
    weights = jnp.exp(scores - peak)
    total = jnp.sum(weights, axis=1, keepdims=True)
    mixed = jnp.dot(weights.astype(jnp.bfloat16), values, preferred_element_type=jnp.float32)
    return mixed / total


def read_tokens(ref, column):
    block = ref[:, :, column : column + LANES]
    n, rows, _ = block.shape
    if rows % 16:
        return block.astype(jnp.float32).reshape(n * rows, LANES).astype(block.dtype)
    return block.reshape(n * rows, LANES)


def write_tokens(ref, column, result):
    n, rows, _ = ref.shape
    ref[:, :, column : column + LANES] = result.reshape(n, rows, LANES).astype(ref.dtype)


def fused_kernel(n, ratio, *refs):
    video_length, audio_length, align_offset = refs[:3]
    arrays = refs[3:15]
    outs = refs[15:19]
    held = refs[19:31]
    results = refs[31:35]
    send_sem, recv_sem, back_send, back_recv = refs[35:]
    me = lax.axis_index("seq")

    def columns(width, owner):
        return pl.ds(pl.multiple_of(owner * width, LANES), width)

    own = []
    for group in GROUPS:
        for at in group:
            width = held[at].shape[2]
            copy = pltpu.make_async_copy(
                arrays[at].at[:, columns(width, me)], held[at].at[me], recv_sem.at[at]
            )
            own.append(copy)
            copy.start()

    barrier = pltpu.get_barrier_semaphore()

    @pl.loop(1, n)
    def _(step):
        pl.semaphore_signal(
            barrier,
            inc=1,
            device_id={"seq": lax.rem(me + step, n)},
            device_id_type=pl.DeviceIdType.MESH,
        )

    pl.semaphore_wait(barrier, n - 1)

    for group in GROUPS:

        @pl.loop(1, n)
        def _(step, group=group):
            peer = lax.rem(me + step, n)
            for at in group:
                width = held[at].shape[2]
                pltpu.make_async_remote_copy(
                    src_ref=arrays[at].at[:, columns(width, peer)],
                    dst_ref=held[at].at[me],
                    send_sem=send_sem.at[at],
                    recv_sem=recv_sem.at[at],
                    device_id={"seq": peer},
                    device_id_type=pl.DeviceIdType.MESH,
                ).start()

    video_valid = video_length[0]
    audio_valid = audio_length[0]
    shift = align_offset[0]
    video_total = n * held[0].shape[1]
    audio_total = n * held[3].shape[1]
    video_reach = video_total // 8
    audio_reach = 5 * audio_total // 8

    def places(count, copies):
        rows = lax.broadcasted_iota(jnp.int32, (count, 1), 0)
        return jnp.concatenate([rows] * copies, axis=0)

    def key_places(count):
        return lax.broadcasted_iota(jnp.int32, (1, count), 1)

    def permit_of(which, copies):
        if which == 0:
            return key_places(video_total) < video_valid
        if which == 1:
            return key_places(audio_total) < audio_valid
        if which == 2:
            where = key_places(audio_total)
            spots = lax.shift_right_logical(places(video_total, copies), ratio.bit_length() - 1)
            center = jnp.clip(spots + shift, 0, audio_valid - 1)
            return (where < audio_valid) & (jnp.abs(where - center) <= audio_reach)
        where = key_places(video_total)
        spots = (places(audio_total, copies) - shift) * ratio
        center = jnp.clip(spots, 0, video_valid - 1)
        return (where < video_valid) & (jnp.abs(where - center) <= video_reach)

    for group, which in zip(GROUPS, OUT_OF_GROUP):
        for at in group:
            pltpu.make_async_copy(held[at], held[at], recv_sem.at[at]).wait()
        query, keys, values = (held[at] for at in group)
        depth = HDV if which == 0 else HDA
        copies = LANES // depth
        scale = 1.0 / math.sqrt(depth)
        permit = permit_of(which, copies)
        for column in range(0, query.shape[2], LANES):
            tokens = read_tokens(query, column)
            if copies > 1:
                lane = lax.broadcasted_iota(jnp.int32, tokens.shape, 1) // depth
                zero = jnp.zeros_like(tokens)
                tokens = jnp.concatenate(
                    [jnp.where(lane == head, tokens, zero) for head in range(copies)], axis=0
                )
            mixed = softmax_mix(
                tokens, read_tokens(keys, column), read_tokens(values, column), permit, scale
            )
            if copies > 1:
                rows = mixed.shape[0] // copies
                merged = mixed[:rows]
                lane = lax.broadcasted_iota(jnp.int32, merged.shape, 1) // depth
                for head in range(1, copies):
                    merged = jnp.where(lane == head, mixed[head * rows : (head + 1) * rows], merged)
                mixed = merged
            write_tokens(results[which], column, mixed)
        width = results[which].shape[2]
        target = outs[which].at[:, columns(width, me)]
        pltpu.make_async_copy(results[which].at[me], target, back_recv.at[which]).start()

        @pl.loop(1, n)
        def _(step, which=which, target=target):
            peer = lax.rem(me + step, n)
            pltpu.make_async_remote_copy(
                src_ref=results[which].at[peer],
                dst_ref=target,
                send_sem=back_send.at[which],
                recv_sem=back_recv.at[which],
                device_id={"seq": peer},
                device_id_type=pl.DeviceIdType.MESH,
            ).start()

    for at in range(12):
        part = held[at].at[pl.ds(0, n - 1)]
        pltpu.make_async_copy(part, part, send_sem.at[at]).wait()
    for which in range(4):
        part = results[which].at[pl.ds(0, n - 1)]
        pltpu.make_async_copy(part, part, back_send.at[which]).wait()
        pltpu.make_async_copy(outs[which], outs[which], back_recv.at[which]).wait()


def fused_shards(*arguments):
    n = lax.axis_size("seq")
    arrays = arguments[:12]
    lengths = arguments[12:]
    ratio = arrays[0].shape[0] // arrays[3].shape[0]
    held = [pltpu.VMEM((n, a.shape[0], a.shape[1] // n), a.dtype) for a in arrays]
    results = [held[at] for at in (0, 3, 6, 9)]
    outs = tuple(jax.ShapeDtypeStruct(arrays[at].shape, arrays[at].dtype) for at in (0, 3, 6, 9))
    anywhere = pl.BlockSpec(memory_space=pl.ANY)
    scalars = pl.BlockSpec(memory_space=pltpu.SMEM)
    return pl.pallas_call(
        functools.partial(fused_kernel, n, ratio),
        out_shape=outs,
        in_specs=[scalars] * 3 + [anywhere] * 12,
        out_specs=(anywhere,) * 4,
        scratch_shapes=held
        + results
        + [
            pltpu.SemaphoreType.DMA((12,)),
            pltpu.SemaphoreType.DMA((12,)),
            pltpu.SemaphoreType.DMA((4,)),
            pltpu.SemaphoreType.DMA((4,)),
        ],
        compiler_params=pltpu.CompilerParams(collective_id=0, has_side_effects=True),
    )(*lengths, *arrays)


def kernel_fits(n, video_rows, audio_rows):
    if n < 2 or HV % n or HA % n or (HV // n * HDV) % LANES or (HA // n * HDA) % LANES:
        return False
    ratio = video_rows // audio_rows
    return video_rows == ratio * audio_rows and ratio & (ratio - 1) == 0 and audio_rows % 8 == 0


def dispatch(*arguments):
    fits = kernel_fits(lax.axis_size("seq"), arguments[0].shape[0], arguments[3].shape[0])
    return (fused_shards if fits else shards)(*arguments)


def solution(mesh):
    placed = (
        P(("clip", "seq"), None),
        P(("clip", "seq"), None),
        P(("clip", "seq"), None),
        P(("clip", "seq"), None),
        P(("clip", "seq"), None),
        P(("clip", "seq"), None),
        P(("clip", "seq"), None),
        P(("clip", "seq"), None),
        P(("clip", "seq"), None),
        P(("clip", "seq"), None),
        P(("clip", "seq"), None),
        P(("clip", "seq"), None),
        P("clip"),
        P("clip"),
        P("clip"),
    )
    return jax.shard_map(
        dispatch,
        mesh=mesh,
        in_specs=placed,
        out_specs=(
            P(("clip", "seq"), None),
            P(("clip", "seq"), None),
            P(("clip", "seq"), None),
            P(("clip", "seq"), None),
        ),
        check_vma=False,
    )
```

```python
import functools
import math

import jax
import jax.numpy as jnp
from jax import lax
from jax.experimental import pallas as pl
from jax.experimental.pallas import tpu as pltpu
from jax.sharding import PartitionSpec as P

HV = 32
HDV = 128
HA = 32
HDA = 64


def block_size(total, limit):
    chosen = min(total, limit)
    while total % chosen:
        chosen -= 1
    return chosen


def split_heads(tokens, heads, depth, copies):
    rows = tokens.shape[0]
    shaped = tokens.reshape(copies, rows // copies, heads, depth).transpose(2, 0, 1, 3)
    return shaped.reshape(heads * copies, rows // copies, depth)


def spread_heads(tokens, heads, depth, copies):
    rows = tokens.shape[0]
    shaped = tokens.reshape(rows, heads, depth).transpose(1, 0, 2)
    shaped = jnp.broadcast_to(shaped[:, None], (heads, copies, rows, depth))
    return shaped.reshape(heads * copies, rows, depth)


def join_heads(owned, heads, depth, copies):
    part_rows = owned.shape[1]
    shaped = owned.reshape(heads, copies, part_rows, depth).transpose(1, 2, 0, 3)
    return shaped.reshape(copies * part_rows, heads * depth)


def owned_positions(rows, copies, devices, index):
    part_rows = rows // copies
    flat = jnp.arange(devices * part_rows, dtype=jnp.int32)
    return flat // part_rows * rows + index % copies * part_rows + flat % part_rows


def online_update(carry, scores, permit, value_tile, value_form):
    running, total, accum = carry
    scores = jnp.where(permit, scores, -1e30)
    newmax = jnp.maximum(running, jnp.max(scores, axis=2))
    weights = jnp.where(permit, jnp.exp(scores - newmax[:, :, None]), 0.0)
    factor = jnp.exp(running - newmax)
    total = total * factor + jnp.sum(weights, axis=2)
    mixed = jnp.einsum(
        value_form, weights.astype(jnp.bfloat16), value_tile, preferred_element_type=jnp.float32
    )
    accum = accum * factor[:, :, None] + mixed
    return (newmax, total, accum)


def fold_initial(rows, heads, depth):
    return (
        jnp.full((heads, rows), -1e30, jnp.float32),
        jnp.zeros((heads, rows), jnp.float32),
        jnp.zeros((heads, rows, depth), jnp.float32),
    )


def fold_piece(carry, local_query, key_rows, value_rows, permit, heads, depth):
    keyed = key_rows.reshape(key_rows.shape[0], heads, depth)
    valued = value_rows.reshape(value_rows.shape[0], heads, depth)
    scores = jnp.einsum("qhd,khd->hqk", local_query, keyed, preferred_element_type=jnp.float32) * (
        1.0 / math.sqrt(depth)
    )
    return online_update(carry, scores, permit[None], valued, "hqk,khd->hqd")


def fold_finish(carry, heads, depth):
    running, total, accum = carry
    result = (accum / total[:, :, None]).astype(jnp.bfloat16)
    return result.transpose(1, 0, 2).reshape(result.shape[1], heads * depth)


def attend_local(queries, keys, values, query_pos, key_pos, allowed):
    heads, q_count, depth = queries.shape
    k_count = keys.shape[1]
    q_block = block_size(q_count, 512)
    k_block = block_size(k_count, 2048)
    scale = 1.0 / math.sqrt(depth)
    q_tiles = queries.reshape(heads, q_count // q_block, q_block, depth).transpose(1, 0, 2, 3)
    k_tiles = keys.reshape(heads, k_count // k_block, k_block, depth).transpose(1, 0, 2, 3)
    v_tiles = values.reshape(heads, k_count // k_block, k_block, depth).transpose(1, 0, 2, 3)
    q_places = query_pos.reshape(q_count // q_block, q_block)
    k_places = key_pos.reshape(k_count // k_block, k_block)

    def one_tile(packed):
        q_tile, q_where = packed

        def absorb(carry, piece):
            k_tile, v_tile, k_where = piece
            scores = (
                jnp.einsum("hqd,hkd->hqk", q_tile, k_tile, preferred_element_type=jnp.float32)
                * scale
            )
            permit = allowed(q_where[:, None], k_where[None, :])[None]
            return (online_update(carry, scores, permit, v_tile, "hqk,hkd->hqd"), None)

        initial = fold_initial(q_block, heads, depth)
        final_state, unused = lax.scan(absorb, initial, (k_tiles, v_tiles, k_places))
        running, total, accum = final_state
        return (accum / total[:, :, None]).astype(jnp.bfloat16)

    tiles = lax.map(one_tile, (q_tiles, q_places))
    return tiles.transpose(1, 0, 2, 3).reshape(heads, q_count, depth)


def shards(
    video_query,
    video_keys,
    video_values,
    audio_query,
    audio_keys,
    audio_values,
    cross_video_query,
    cross_video_keys,
    cross_video_values,
    cross_audio_query,
    cross_audio_keys,
    cross_audio_values,
    video_length,
    audio_length,
    align_offset,
):
    devices = lax.axis_size("seq")
    index = lax.axis_index("seq")
    video_rows = video_query.shape[0]
    audio_rows = audio_query.shape[0]
    video_total = video_rows * devices
    audio_total = audio_rows * devices
    video_reach = video_total // 8
    audio_reach = 5 * audio_total // 8
    video_valid = video_length[0]
    audio_valid = audio_length[0]
    align_shift = align_offset[0]
    copies = max(devices // HV, 1)
    video_places = jnp.arange(video_total, dtype=jnp.int32)
    audio_places = jnp.arange(audio_total, dtype=jnp.int32)

    def video_open(q_where, k_where):
        return k_where < video_valid

    def toward_video(q_where, k_where):
        center = jnp.clip(q_where * audio_total // video_total + align_shift, 0, audio_valid - 1)
        return (k_where < audio_valid) & (jnp.abs(k_where - center) <= audio_reach)

    def toward_audio(q_where, k_where):
        center = jnp.clip((q_where - align_shift) * video_total // audio_total, 0, video_valid - 1)
        return (k_where < video_valid) & (jnp.abs(k_where - center) <= video_reach)

    video_owned = (
        lax.all_to_all(
            split_heads(video_query, HV, HDV, copies),
            "seq",
            split_axis=0,
            concat_axis=1,
            tiled=True,
        ),
        lax.all_to_all(
            spread_heads(video_keys, HV, HDV, copies),
            "seq",
            split_axis=0,
            concat_axis=1,
            tiled=True,
        ),
        lax.all_to_all(
            spread_heads(video_values, HV, HDV, copies),
            "seq",
            split_axis=0,
            concat_axis=1,
            tiled=True,
        ),
    )
    video_done = attend_local(
        video_owned[0],
        video_owned[1],
        video_owned[2],
        owned_positions(video_rows, copies, devices, index),
        video_places,
        video_open,
    )
    video_mixed = join_heads(
        lax.all_to_all(video_done, "seq", split_axis=1, concat_axis=0, tiled=True), HV, HDV, copies
    )
    audio_local = audio_query.reshape(audio_rows, HA, HDA)
    piece = (
        lax.all_gather(audio_keys, "seq", axis=0, tiled=True),
        lax.all_gather(audio_values, "seq", axis=0, tiled=True),
    )
    k_where = jnp.arange(piece[0].shape[0], dtype=jnp.int32)
    audio_k_where = k_where[None, :]
    permit = audio_k_where < audio_valid
    audio_state = fold_piece(
        fold_initial(audio_rows, HA, HDA), audio_local, piece[0], piece[1], permit, HA, HDA
    )
    audio_mixed = fold_finish(audio_state, HA, HDA)
    cross_owned = (
        lax.all_to_all(
            split_heads(cross_video_query, HA, HDA, copies),
            "seq",
            split_axis=0,
            concat_axis=1,
            tiled=True,
        ),
        lax.all_to_all(
            spread_heads(cross_audio_keys, HA, HDA, copies),
            "seq",
            split_axis=0,
            concat_axis=1,
            tiled=True,
        ),
        lax.all_to_all(
            spread_heads(cross_audio_values, HA, HDA, copies),
            "seq",
            split_axis=0,
            concat_axis=1,
            tiled=True,
        ),
    )
    cross_done = attend_local(
        cross_owned[0],
        cross_owned[1],
        cross_owned[2],
        owned_positions(video_rows, copies, devices, index),
        audio_places,
        toward_video,
    )
    video_cross = join_heads(
        lax.all_to_all(cross_done, "seq", split_axis=1, concat_axis=0, tiled=True), HA, HDA, copies
    )
    listen_owned = (
        lax.all_to_all(
            split_heads(cross_audio_query, HA, HDA, copies),
            "seq",
            split_axis=0,
            concat_axis=1,
            tiled=True,
        ),
        lax.all_to_all(
            spread_heads(cross_video_keys, HA, HDA, copies),
            "seq",
            split_axis=0,
            concat_axis=1,
            tiled=True,
        ),
        lax.all_to_all(
            spread_heads(cross_video_values, HA, HDA, copies),
            "seq",
            split_axis=0,
            concat_axis=1,
            tiled=True,
        ),
    )
    listen_done = attend_local(
        listen_owned[0],
        listen_owned[1],
        listen_owned[2],
        owned_positions(audio_rows, copies, devices, index),
        video_places,
        toward_audio,
    )
    audio_cross = join_heads(
        lax.all_to_all(listen_done, "seq", split_axis=1, concat_axis=0, tiled=True), HA, HDA, copies
    )
    return (video_mixed, audio_mixed, video_cross, audio_cross)


LANES = 128

GROUPS = (
    ((0, 1, 2), 0, False),
    ((3, 4, 5), 1, False),
    ((9, 7, 8), 3, True),
    ((6, 10, 11), 2, True),
)


def softmax_mix(query, keys, values, permit, scale):
    scores = lax.dot_general(
        query, keys, (((1,), (1,)), ((), ())), preferred_element_type=jnp.float32
    )
    scores = jnp.where(permit, scores * scale, -1e30)
    peak = jnp.max(scores, axis=1, keepdims=True)
    weights = jnp.exp(scores - peak)
    total = jnp.sum(weights, axis=1, keepdims=True)
    mixed = jnp.dot(weights.astype(jnp.bfloat16), values, preferred_element_type=jnp.float32)
    return mixed / total


def read_tokens(ref, column):
    block = ref[:, :, column : column + LANES]
    n, rows, _ = block.shape
    if rows % 16:
        return block.astype(jnp.float32).reshape(n * rows, LANES).astype(block.dtype)
    return block.reshape(n * rows, LANES)


def write_tokens(ref, column, result):
    n, rows, _ = ref.shape
    ref[:, :, column : column + LANES] = result.reshape(n, rows, LANES).astype(ref.dtype)


def margin_blocks(n, video_rows):
    return min(-(-(3 * n * video_rows // 16) // video_rows), n // 2)


def held_shapes(n, arrays):
    half = n // 2
    shapes = [None] * 12
    for group, which, halved in GROUPS:
        for place, at in enumerate(group):
            rows, cols = arrays[at].shape
            blocks = n
            if halved and place == 0:
                blocks = half
            elif which == 3:
                blocks = half + margin_blocks(n, rows)
            shapes[at] = (blocks, rows, cols // (half if halved else n))
    return shapes


def fused_kernel(n, ratio, *refs):
    video_length, audio_length, align_offset = refs[:3]
    arrays = refs[3:15]
    outs = refs[15:19]
    held = refs[19:31]
    results = refs[31:35]
    send_sem, far_sem, recv_sem, back_send, back_recv = refs[35:]
    half = n // 2
    margin = held[7].shape[0] - half
    me = lax.axis_index("seq")
    side = me // half
    inner = lax.rem(me, half)
    near = (me >= half - margin) & (me < half + margin)

    def columns(width, owner):
        return pl.ds(pl.multiple_of(owner * width, LANES), width)

    def slot_of(group, which, halved, at, to_side):
        if halved and at == group[0]:
            return inner
        if which == 3:
            return me - to_side * (half - margin)
        return me

    def send(at, owner, slot, peer, sem):
        pltpu.make_async_remote_copy(
            src_ref=arrays[at].at[:, columns(held[at].shape[2], owner)],
            dst_ref=held[at].at[slot],
            send_sem=sem.at[at],
            recv_sem=recv_sem.at[at],
            device_id={"seq": peer},
            device_id_type=pl.DeviceIdType.MESH,
        ).start()

    for group, which, halved in GROUPS:
        for at in group:
            pltpu.make_async_copy(
                arrays[at].at[:, columns(held[at].shape[2], inner if halved else me)],
                held[at].at[slot_of(group, which, halved, at, side)],
                recv_sem.at[at],
            ).start()

    barrier = pltpu.get_barrier_semaphore()

    @pl.loop(1, n)
    def _(step):
        pl.semaphore_signal(
            barrier,
            inc=1,
            device_id={"seq": lax.rem(me + step, n)},
            device_id_type=pl.DeviceIdType.MESH,
        )

    pl.semaphore_wait(barrier, n - 1)

    for group, which, halved in GROUPS:
        if not halved:

            @pl.loop(0, half)
            def _(step, group=group):
                peer = (1 - side) * half + lax.rem(inner + step, half)
                for at in group:
                    send(at, peer, me, peer, far_sem)

            @pl.loop(1, half)
            def _(step, group=group):
                peer = side * half + lax.rem(inner + step, half)
                for at in group:
                    send(at, peer, me, peer, send_sem)

            continue

        def far_sends(group=group, which=which):
            @pl.loop(0, half)
            def _(step):
                owner = lax.rem(inner + step, half)
                for at in group[1:]:
                    slot = slot_of(group, which, True, at, 1 - side)
                    send(at, owner, slot, (1 - side) * half + owner, far_sem)

        if which == 3:
            pl.when(near)(far_sends)
        else:
            far_sends()

        @pl.loop(1, half)
        def _(step, group=group, which=which):
            owner = lax.rem(inner + step, half)
            for at in group:
                slot = slot_of(group, which, True, at, side)
                send(at, owner, slot, side * half + owner, send_sem)

    video_valid = video_length[0]
    audio_valid = audio_length[0]
    shift = align_offset[0]
    video_rows = arrays[0].shape[0]
    audio_rows = arrays[3].shape[0]
    video_total = n * video_rows
    audio_total = n * audio_rows
    video_reach = video_total // 8
    audio_reach = 5 * audio_total // 8

    def query_places(count, copies, first):
        rows = first + lax.broadcasted_iota(jnp.int32, (count, 1), 0)
        return jnp.concatenate([rows] * copies, axis=0)

    def key_places(count):
        return lax.broadcasted_iota(jnp.int32, (1, count), 1)

    def permit_of(which, copies):
        if which == 0:
            return key_places(video_total) < video_valid
        if which == 1:
            return key_places(audio_total) < audio_valid
        if which == 2:
            where = key_places(audio_total)
            spots = query_places(half * video_rows, copies, side * half * video_rows)
            spots = lax.shift_right_logical(spots, ratio.bit_length() - 1)
            center = jnp.clip(spots + shift, 0, audio_valid - 1)
            return (where < audio_valid) & (jnp.abs(where - center) <= audio_reach)
        where = key_places((half + margin) * video_rows) + side * (half - margin) * video_rows
        spots = query_places(half * audio_rows, copies, side * half * audio_rows)
        center = jnp.clip((spots - shift) * ratio, 0, video_valid - 1)
        return (where < video_valid) & (jnp.abs(where - center) <= video_reach)

    for group, which, halved in GROUPS:
        for at in group:
            pltpu.make_async_copy(held[at], held[at], recv_sem.at[at]).wait()
        query, keys, values = (held[at] for at in group)
        depth = HDV if which == 0 else HDA
        copies = LANES // depth
        scale = 1.0 / math.sqrt(depth)
        permit = permit_of(which, copies)
        for column in range(0, query.shape[2], LANES):
            tokens = read_tokens(query, column)
            if copies > 1:
                lane = lax.broadcasted_iota(jnp.int32, tokens.shape, 1) // depth
                zero = jnp.zeros_like(tokens)
                tokens = jnp.concatenate(
                    [jnp.where(lane == head, tokens, zero) for head in range(copies)], axis=0
                )
            mixed = softmax_mix(
                tokens, read_tokens(keys, column), read_tokens(values, column), permit, scale
            )
            if copies > 1:
                rows = mixed.shape[0] // copies
                merged = mixed[:rows]
                lane = lax.broadcasted_iota(jnp.int32, merged.shape, 1) // depth
                for head in range(1, copies):
                    merged = jnp.where(lane == head, mixed[head * rows : (head + 1) * rows], merged)
                mixed = merged
            write_tokens(results[which], column, mixed)
        mine = inner if halved else me
        count = half if halved else n
        first = side * half if halved else 0
        target = outs[which].at[:, columns(results[which].shape[2], mine)]
        pltpu.make_async_copy(results[which].at[mine], target, back_recv.at[which]).start()

        @pl.loop(1, count)
        def _(step, which=which, target=target, mine=mine, count=count, first=first):
            block = lax.rem(mine + step, count)
            pltpu.make_async_remote_copy(
                src_ref=results[which].at[block],
                dst_ref=target,
                send_sem=back_send.at[which],
                recv_sem=back_recv.at[which],
                device_id={"seq": first + block},
                device_id_type=pl.DeviceIdType.MESH,
            ).start()

    def wait_bytes(ref, blocks, sem):
        part = ref.at[pl.ds(0, blocks)]
        pltpu.make_async_copy(part, part, sem).wait()

    for group, which, halved in GROUPS:
        for at in group:
            wait_bytes(held[at], half - 1, send_sem.at[at])
            if not halved or (which == 2 and at != group[0]):
                wait_bytes(held[at], half, far_sem.at[at])
            elif at != group[0]:

                @pl.when(near)
                def _(at=at):
                    wait_bytes(held[at], half, far_sem.at[at])

    for which in range(4):
        wait_bytes(results[which], results[which].shape[0] - 1, back_send.at[which])
        pltpu.make_async_copy(outs[which], outs[which], back_recv.at[which]).wait()


def write_out(*refs):
    sources, targets, sem = refs[:4], refs[4:8], refs[8]
    copies = [pltpu.make_async_copy(*pair, sem.at[at]) for at, pair in enumerate(zip(sources, targets))]
    for copy in copies:
        copy.start()
    for copy in copies:
        copy.wait()


def fused_shards(*arguments):
    n = lax.axis_size("seq")
    arrays = arguments[:12]
    lengths = arguments[12:]
    arrays = [pltpu.with_memory_space_constraint(a, pltpu.HBM) for a in arrays]
    ratio = arrays[0].shape[0] // arrays[3].shape[0]
    held = [pltpu.VMEM(s, a.dtype) for s, a in zip(held_shapes(n, arrays), arrays)]
    results = [
        pltpu.VMEM((n, *held[0].shape[1:]), jnp.bfloat16),
        pltpu.VMEM((n, *held[3].shape[1:]), jnp.bfloat16),
        pltpu.VMEM((n // 2, *held[6].shape[1:]), jnp.bfloat16),
        pltpu.VMEM((n // 2, *held[9].shape[1:]), jnp.bfloat16),
    ]
    shapes = [arrays[at].shape for at in (0, 3, 6, 9)]
    anywhere = pl.BlockSpec(memory_space=pl.ANY)
    scalars = pl.BlockSpec(memory_space=pltpu.SMEM)
    vectors = pl.BlockSpec(memory_space=pltpu.VMEM)
    mixed = pl.pallas_call(
        functools.partial(fused_kernel, n, ratio),
        out_shape=tuple(pltpu.VMEM(shape, jnp.bfloat16) for shape in shapes),
        in_specs=[scalars] * 3 + [pl.BlockSpec(memory_space=pltpu.HBM)] * 12,
        out_specs=(vectors,) * 4,
        scratch_shapes=held
        + results
        + [
            pltpu.SemaphoreType.DMA((12,)),
            pltpu.SemaphoreType.DMA((12,)),
            pltpu.SemaphoreType.DMA((12,)),
            pltpu.SemaphoreType.DMA((4,)),
            pltpu.SemaphoreType.DMA((4,)),
        ],
        compiler_params=pltpu.CompilerParams(
            collective_id=0, has_side_effects=True, vmem_limit_bytes=24 * 2**20
        ),
    )(*lengths, *arrays)
    return pl.pallas_call(
        write_out,
        out_shape=tuple(jax.ShapeDtypeStruct(shape, jnp.bfloat16) for shape in shapes),
        in_specs=[vectors] * 4,
        out_specs=(anywhere,) * 4,
        scratch_shapes=[pltpu.SemaphoreType.DMA((4,))],
        compiler_params=pltpu.CompilerParams(vmem_limit_bytes=2**20),
    )(*mixed)


def kernel_fits(n, video_rows, audio_rows):
    if n < 4 or n % 2 or HV % n or HA % n or (HV // n * HDV) % LANES or (HA // n * HDA) % LANES:
        return False
    ratio = video_rows // audio_rows
    return video_rows == ratio * audio_rows and ratio & (ratio - 1) == 0 and n * audio_rows % 16 == 0 and audio_rows % 8 == 0


def dispatch(*arguments):
    fits = kernel_fits(lax.axis_size("seq"), arguments[0].shape[0], arguments[3].shape[0])
    return (fused_shards if fits else shards)(*arguments)


def solution(mesh):
    placed = (
        P(("clip", "seq"), None),
        P(("clip", "seq"), None),
        P(("clip", "seq"), None),
        P(("clip", "seq"), None),
        P(("clip", "seq"), None),
        P(("clip", "seq"), None),
        P(("clip", "seq"), None),
        P(("clip", "seq"), None),
        P(("clip", "seq"), None),
        P(("clip", "seq"), None),
        P(("clip", "seq"), None),
        P(("clip", "seq"), None),
        P("clip"),
        P("clip"),
        P("clip"),
    )
    return jax.shard_map(
        dispatch,
        mesh=mesh,
        in_specs=placed,
        out_specs=(
            P(("clip", "seq"), None),
            P(("clip", "seq"), None),
            P(("clip", "seq"), None),
            P(("clip", "seq"), None),
        ),
        check_vma=False,
    )
```

```python
import functools
import math

import jax
import jax.numpy as jnp
from jax import lax
from jax.experimental import pallas as pl
from jax.experimental.pallas import tpu as pltpu
from jax.sharding import PartitionSpec as P

HV = 32
HDV = 128
HA = 32
HDA = 64


def block_size(total, limit):
    chosen = min(total, limit)
    while total % chosen:
        chosen -= 1
    return chosen


def split_heads(tokens, heads, depth, copies):
    rows = tokens.shape[0]
    shaped = tokens.reshape(copies, rows // copies, heads, depth).transpose(2, 0, 1, 3)
    return shaped.reshape(heads * copies, rows // copies, depth)


def spread_heads(tokens, heads, depth, copies):
    rows = tokens.shape[0]
    shaped = tokens.reshape(rows, heads, depth).transpose(1, 0, 2)
    shaped = jnp.broadcast_to(shaped[:, None], (heads, copies, rows, depth))
    return shaped.reshape(heads * copies, rows, depth)


def join_heads(owned, heads, depth, copies):
    part_rows = owned.shape[1]
    shaped = owned.reshape(heads, copies, part_rows, depth).transpose(1, 2, 0, 3)
    return shaped.reshape(copies * part_rows, heads * depth)


def owned_positions(rows, copies, devices, index):
    part_rows = rows // copies
    flat = jnp.arange(devices * part_rows, dtype=jnp.int32)
    return flat // part_rows * rows + index % copies * part_rows + flat % part_rows


def online_update(carry, scores, permit, value_tile, value_form):
    running, total, accum = carry
    scores = jnp.where(permit, scores, -1e30)
    newmax = jnp.maximum(running, jnp.max(scores, axis=2))
    weights = jnp.where(permit, jnp.exp(scores - newmax[:, :, None]), 0.0)
    factor = jnp.exp(running - newmax)
    total = total * factor + jnp.sum(weights, axis=2)
    mixed = jnp.einsum(
        value_form, weights.astype(jnp.bfloat16), value_tile, preferred_element_type=jnp.float32
    )
    accum = accum * factor[:, :, None] + mixed
    return (newmax, total, accum)


def fold_initial(rows, heads, depth):
    return (
        jnp.full((heads, rows), -1e30, jnp.float32),
        jnp.zeros((heads, rows), jnp.float32),
        jnp.zeros((heads, rows, depth), jnp.float32),
    )


def fold_piece(carry, local_query, key_rows, value_rows, permit, heads, depth):
    keyed = key_rows.reshape(key_rows.shape[0], heads, depth)
    valued = value_rows.reshape(value_rows.shape[0], heads, depth)
    scores = jnp.einsum("qhd,khd->hqk", local_query, keyed, preferred_element_type=jnp.float32) * (
        1.0 / math.sqrt(depth)
    )
    return online_update(carry, scores, permit[None], valued, "hqk,khd->hqd")


def fold_finish(carry, heads, depth):
    running, total, accum = carry
    result = (accum / total[:, :, None]).astype(jnp.bfloat16)
    return result.transpose(1, 0, 2).reshape(result.shape[1], heads * depth)


def attend_local(queries, keys, values, query_pos, key_pos, allowed):
    heads, q_count, depth = queries.shape
    k_count = keys.shape[1]
    q_block = block_size(q_count, 512)
    k_block = block_size(k_count, 2048)
    scale = 1.0 / math.sqrt(depth)
    q_tiles = queries.reshape(heads, q_count // q_block, q_block, depth).transpose(1, 0, 2, 3)
    k_tiles = keys.reshape(heads, k_count // k_block, k_block, depth).transpose(1, 0, 2, 3)
    v_tiles = values.reshape(heads, k_count // k_block, k_block, depth).transpose(1, 0, 2, 3)
    q_places = query_pos.reshape(q_count // q_block, q_block)
    k_places = key_pos.reshape(k_count // k_block, k_block)

    def one_tile(packed):
        q_tile, q_where = packed

        def absorb(carry, piece):
            k_tile, v_tile, k_where = piece
            scores = (
                jnp.einsum("hqd,hkd->hqk", q_tile, k_tile, preferred_element_type=jnp.float32)
                * scale
            )
            permit = allowed(q_where[:, None], k_where[None, :])[None]
            return (online_update(carry, scores, permit, v_tile, "hqk,hkd->hqd"), None)

        initial = fold_initial(q_block, heads, depth)
        final_state, unused = lax.scan(absorb, initial, (k_tiles, v_tiles, k_places))
        running, total, accum = final_state
        return (accum / total[:, :, None]).astype(jnp.bfloat16)

    tiles = lax.map(one_tile, (q_tiles, q_places))
    return tiles.transpose(1, 0, 2, 3).reshape(heads, q_count, depth)


def shards(
    video_query,
    video_keys,
    video_values,
    audio_query,
    audio_keys,
    audio_values,
    cross_video_query,
    cross_video_keys,
    cross_video_values,
    cross_audio_query,
    cross_audio_keys,
    cross_audio_values,
    video_length,
    audio_length,
    align_offset,
):
    devices = lax.axis_size("seq")
    index = lax.axis_index("seq")
    video_rows = video_query.shape[0]
    audio_rows = audio_query.shape[0]
    video_total = video_rows * devices
    audio_total = audio_rows * devices
    video_reach = video_total // 8
    audio_reach = 5 * audio_total // 8
    video_valid = video_length[0]
    audio_valid = audio_length[0]
    align_shift = align_offset[0]
    copies = max(devices // HV, 1)
    video_places = jnp.arange(video_total, dtype=jnp.int32)
    audio_places = jnp.arange(audio_total, dtype=jnp.int32)

    def video_open(q_where, k_where):
        return k_where < video_valid

    def toward_video(q_where, k_where):
        center = jnp.clip(q_where * audio_total // video_total + align_shift, 0, audio_valid - 1)
        return (k_where < audio_valid) & (jnp.abs(k_where - center) <= audio_reach)

    def toward_audio(q_where, k_where):
        center = jnp.clip((q_where - align_shift) * video_total // audio_total, 0, video_valid - 1)
        return (k_where < video_valid) & (jnp.abs(k_where - center) <= video_reach)

    video_owned = (
        lax.all_to_all(
            split_heads(video_query, HV, HDV, copies),
            "seq",
            split_axis=0,
            concat_axis=1,
            tiled=True,
        ),
        lax.all_to_all(
            spread_heads(video_keys, HV, HDV, copies),
            "seq",
            split_axis=0,
            concat_axis=1,
            tiled=True,
        ),
        lax.all_to_all(
            spread_heads(video_values, HV, HDV, copies),
            "seq",
            split_axis=0,
            concat_axis=1,
            tiled=True,
        ),
    )
    video_done = attend_local(
        video_owned[0],
        video_owned[1],
        video_owned[2],
        owned_positions(video_rows, copies, devices, index),
        video_places,
        video_open,
    )
    video_mixed = join_heads(
        lax.all_to_all(video_done, "seq", split_axis=1, concat_axis=0, tiled=True), HV, HDV, copies
    )
    audio_local = audio_query.reshape(audio_rows, HA, HDA)
    piece = (
        lax.all_gather(audio_keys, "seq", axis=0, tiled=True),
        lax.all_gather(audio_values, "seq", axis=0, tiled=True),
    )
    k_where = jnp.arange(piece[0].shape[0], dtype=jnp.int32)
    audio_k_where = k_where[None, :]
    permit = audio_k_where < audio_valid
    audio_state = fold_piece(
        fold_initial(audio_rows, HA, HDA), audio_local, piece[0], piece[1], permit, HA, HDA
    )
    audio_mixed = fold_finish(audio_state, HA, HDA)
    cross_owned = (
        lax.all_to_all(
            split_heads(cross_video_query, HA, HDA, copies),
            "seq",
            split_axis=0,
            concat_axis=1,
            tiled=True,
        ),
        lax.all_to_all(
            spread_heads(cross_audio_keys, HA, HDA, copies),
            "seq",
            split_axis=0,
            concat_axis=1,
            tiled=True,
        ),
        lax.all_to_all(
            spread_heads(cross_audio_values, HA, HDA, copies),
            "seq",
            split_axis=0,
            concat_axis=1,
            tiled=True,
        ),
    )
    cross_done = attend_local(
        cross_owned[0],
        cross_owned[1],
        cross_owned[2],
        owned_positions(video_rows, copies, devices, index),
        audio_places,
        toward_video,
    )
    video_cross = join_heads(
        lax.all_to_all(cross_done, "seq", split_axis=1, concat_axis=0, tiled=True), HA, HDA, copies
    )
    listen_owned = (
        lax.all_to_all(
            split_heads(cross_audio_query, HA, HDA, copies),
            "seq",
            split_axis=0,
            concat_axis=1,
            tiled=True,
        ),
        lax.all_to_all(
            spread_heads(cross_video_keys, HA, HDA, copies),
            "seq",
            split_axis=0,
            concat_axis=1,
            tiled=True,
        ),
        lax.all_to_all(
            spread_heads(cross_video_values, HA, HDA, copies),
            "seq",
            split_axis=0,
            concat_axis=1,
            tiled=True,
        ),
    )
    listen_done = attend_local(
        listen_owned[0],
        listen_owned[1],
        listen_owned[2],
        owned_positions(audio_rows, copies, devices, index),
        video_places,
        toward_audio,
    )
    audio_cross = join_heads(
        lax.all_to_all(listen_done, "seq", split_axis=1, concat_axis=0, tiled=True), HA, HDA, copies
    )
    return (video_mixed, audio_mixed, video_cross, audio_cross)


LANES = 128

GROUPS = (
    ((0, 1, 2), 0, False),
    ((3, 4, 5), 1, False),
    ((6, 10, 11), 2, True),
    ((9, 7, 8), 3, True),
)


def softmax_mix(query, keys, values, permit, scale):
    scores = lax.dot_general(
        query, keys, (((1,), (1,)), ((), ())), preferred_element_type=jnp.float32
    )
    scores = jnp.where(permit, scores * scale, -1e30)
    peak = jnp.max(scores, axis=1, keepdims=True)
    weights = jnp.exp(scores - peak)
    total = jnp.sum(weights, axis=1, keepdims=True)
    mixed = jnp.dot(weights.astype(jnp.bfloat16), values, preferred_element_type=jnp.float32)
    return mixed / total


def read_tokens(ref, column):
    block = ref[:, :, column : column + LANES]
    n, rows, _ = block.shape
    if rows % 16:
        return block.astype(jnp.float32).reshape(n * rows, LANES).astype(block.dtype)
    return block.reshape(n * rows, LANES)


def write_tokens(ref, column, result):
    n, rows, _ = ref.shape
    ref[:, :, column : column + LANES] = result.reshape(n, rows, LANES).astype(ref.dtype)


def margin_blocks(n, video_rows):
    return min(-(-(3 * n * video_rows // 16) // video_rows), n // 2)


def held_shapes(n, arrays):
    half = n // 2
    shapes = [None] * 12
    for group, which, halved in GROUPS:
        for place, at in enumerate(group):
            rows, cols = arrays[at].shape
            blocks = n
            if halved and place == 0:
                blocks = half
            elif which == 3:
                blocks = half + margin_blocks(n, rows)
            shapes[at] = (blocks, rows, cols // (half if halved else n))
    return shapes


def fused_kernel(n, ratio, *refs):
    video_length, audio_length, align_offset = refs[:3]
    arrays = refs[3:15]
    outs = refs[15:19]
    held = refs[19:31]
    results = refs[31:35]
    send_sem, far_sem, recv_sem, back_send, back_recv = refs[35:]
    half = n // 2
    margin = held[7].shape[0] - half
    me = lax.axis_index("seq")
    side = me // half
    inner = lax.rem(me, half)
    near = (me >= half - margin) & (me < half + margin)

    def columns(width, owner):
        return pl.ds(pl.multiple_of(owner * width, LANES), width)

    def slot_of(group, which, halved, at, to_side):
        if halved and at == group[0]:
            return inner
        if which == 3:
            return me - to_side * (half - margin)
        return me

    def send(at, owner, slot, peer, sem):
        pltpu.make_async_remote_copy(
            src_ref=arrays[at].at[:, columns(held[at].shape[2], owner)],
            dst_ref=held[at].at[slot],
            send_sem=sem.at[at],
            recv_sem=recv_sem.at[at],
            device_id={"seq": peer},
            device_id_type=pl.DeviceIdType.MESH,
        ).start()

    for group, which, halved in GROUPS:
        for at in group:
            pltpu.make_async_copy(
                arrays[at].at[:, columns(held[at].shape[2], inner if halved else me)],
                held[at].at[slot_of(group, which, halved, at, side)],
                recv_sem.at[at],
            ).start()

    barrier = pltpu.get_barrier_semaphore()

    @pl.loop(1, n)
    def _(step):
        pl.semaphore_signal(
            barrier,
            inc=1,
            device_id={"seq": lax.rem(me + step, n)},
            device_id_type=pl.DeviceIdType.MESH,
        )

    pl.semaphore_wait(barrier, n - 1)

    for group, which, halved in GROUPS:
        if not halved:

            @pl.loop(0, half)
            def _(step, group=group):
                peer = (1 - side) * half + lax.rem(inner + step, half)
                for at in group:
                    send(at, peer, me, peer, far_sem)

            @pl.loop(1, half)
            def _(step, group=group):
                peer = side * half + lax.rem(inner + step, half)
                for at in group:
                    send(at, peer, me, peer, send_sem)

            continue

        def far_sends(group=group, which=which):
            @pl.loop(0, half)
            def _(step):
                owner = lax.rem(inner + step, half)
                for at in group[1:]:
                    slot = slot_of(group, which, True, at, 1 - side)
                    send(at, owner, slot, (1 - side) * half + owner, far_sem)

        if which == 3:
            pl.when(near)(far_sends)
        else:
            far_sends()

        @pl.loop(1, half)
        def _(step, group=group, which=which):
            owner = lax.rem(inner + step, half)
            for at in group:
                slot = slot_of(group, which, True, at, side)
                send(at, owner, slot, side * half + owner, send_sem)

    video_valid = video_length[0]
    audio_valid = audio_length[0]
    shift = align_offset[0]
    video_rows = arrays[0].shape[0]
    audio_rows = arrays[3].shape[0]
    video_total = n * video_rows
    audio_total = n * audio_rows
    video_reach = video_total // 8
    audio_reach = 5 * audio_total // 8

    def query_places(count, copies, first):
        rows = first + lax.broadcasted_iota(jnp.int32, (count, 1), 0)
        return jnp.concatenate([rows] * copies, axis=0)

    def key_places(count):
        return lax.broadcasted_iota(jnp.int32, (1, count), 1)

    def permit_of(which, copies):
        if which == 0:
            return key_places(video_total) < video_valid
        if which == 1:
            return key_places(audio_total) < audio_valid
        if which == 2:
            where = key_places(audio_total)
            spots = query_places(half * video_rows, copies, side * half * video_rows)
            spots = lax.shift_right_logical(spots, ratio.bit_length() - 1)
            center = jnp.clip(spots + shift, 0, audio_valid - 1)
            return (where < audio_valid) & (jnp.abs(where - center) <= audio_reach)
        where = key_places((half + margin) * video_rows) + side * (half - margin) * video_rows
        spots = query_places(half * audio_rows, copies, side * half * audio_rows)
        center = jnp.clip((spots - shift) * ratio, 0, video_valid - 1)
        return (where < video_valid) & (jnp.abs(where - center) <= video_reach)

    for group, which, halved in GROUPS:
        for at in group:
            pltpu.make_async_copy(held[at], held[at], recv_sem.at[at]).wait()
        query, keys, values = (held[at] for at in group)
        depth = HDV if which == 0 else HDA
        copies = LANES // depth
        scale = 1.0 / math.sqrt(depth)
        permit = permit_of(which, copies)
        for column in range(0, query.shape[2], LANES):
            tokens = read_tokens(query, column)
            if copies > 1:
                lane = lax.broadcasted_iota(jnp.int32, tokens.shape, 1) // depth
                zero = jnp.zeros_like(tokens)
                tokens = jnp.concatenate(
                    [jnp.where(lane == head, tokens, zero) for head in range(copies)], axis=0
                )
            mixed = softmax_mix(
                tokens, read_tokens(keys, column), read_tokens(values, column), permit, scale
            )
            if copies > 1:
                rows = mixed.shape[0] // copies
                merged = mixed[:rows]
                lane = lax.broadcasted_iota(jnp.int32, merged.shape, 1) // depth
                for head in range(1, copies):
                    merged = jnp.where(lane == head, mixed[head * rows : (head + 1) * rows], merged)
                mixed = merged
            write_tokens(results[which], column, mixed)
        mine = inner if halved else me
        count = half if halved else n
        first = side * half if halved else 0
        target = outs[which].at[:, columns(results[which].shape[2], mine)]
        pltpu.make_async_copy(results[which].at[mine], target, back_recv.at[which]).start()

        @pl.loop(1, count)
        def _(step, which=which, target=target, mine=mine, count=count, first=first):
            block = lax.rem(mine + step, count)
            pltpu.make_async_remote_copy(
                src_ref=results[which].at[block],
                dst_ref=target,
                send_sem=back_send.at[which],
                recv_sem=back_recv.at[which],
                device_id={"seq": first + block},
                device_id_type=pl.DeviceIdType.MESH,
            ).start()

    def wait_bytes(ref, blocks, sem):
        part = ref.at[pl.ds(0, blocks)]
        pltpu.make_async_copy(part, part, sem).wait()

    for group, which, halved in GROUPS:
        for at in group:
            wait_bytes(held[at], half - 1, send_sem.at[at])
            if not halved or (which == 2 and at != group[0]):
                wait_bytes(held[at], half, far_sem.at[at])
            elif at != group[0]:

                @pl.when(near)
                def _(at=at):
                    wait_bytes(held[at], half, far_sem.at[at])

    for which in range(4):
        wait_bytes(results[which], results[which].shape[0] - 1, back_send.at[which])
        pltpu.make_async_copy(outs[which], outs[which], back_recv.at[which]).wait()


def write_out(*refs):
    sources, targets, sem = refs[:4], refs[4:8], refs[8]
    copies = [pltpu.make_async_copy(*pair, sem.at[at]) for at, pair in enumerate(zip(sources, targets))]
    for copy in copies:
        copy.start()
    for copy in copies:
        copy.wait()


def fused_shards(*arguments):
    n = lax.axis_size("seq")
    arrays = arguments[:12]
    lengths = arguments[12:]
    arrays = [pltpu.with_memory_space_constraint(a, pltpu.HBM) for a in arrays]
    ratio = arrays[0].shape[0] // arrays[3].shape[0]
    held = [pltpu.VMEM(s, a.dtype) for s, a in zip(held_shapes(n, arrays), arrays)]
    results = [
        pltpu.VMEM((n, *held[0].shape[1:]), jnp.bfloat16),
        pltpu.VMEM((n, *held[3].shape[1:]), jnp.bfloat16),
        pltpu.VMEM((n // 2, *held[6].shape[1:]), jnp.bfloat16),
        pltpu.VMEM((n // 2, *held[9].shape[1:]), jnp.bfloat16),
    ]
    shapes = [arrays[at].shape for at in (0, 3, 6, 9)]
    anywhere = pl.BlockSpec(memory_space=pl.ANY)
    scalars = pl.BlockSpec(memory_space=pltpu.SMEM)
    vectors = pl.BlockSpec(memory_space=pltpu.VMEM)
    mixed = pl.pallas_call(
        functools.partial(fused_kernel, n, ratio),
        out_shape=tuple(pltpu.VMEM(shape, jnp.bfloat16) for shape in shapes),
        in_specs=[scalars] * 3 + [pl.BlockSpec(memory_space=pltpu.HBM)] * 12,
        out_specs=(vectors,) * 4,
        scratch_shapes=held
        + results
        + [
            pltpu.SemaphoreType.DMA((12,)),
            pltpu.SemaphoreType.DMA((12,)),
            pltpu.SemaphoreType.DMA((12,)),
            pltpu.SemaphoreType.DMA((4,)),
            pltpu.SemaphoreType.DMA((4,)),
        ],
        compiler_params=pltpu.CompilerParams(
            collective_id=0, has_side_effects=True, vmem_limit_bytes=24 * 2**20
        ),
    )(*lengths, *arrays)
    return pl.pallas_call(
        write_out,
        out_shape=tuple(jax.ShapeDtypeStruct(shape, jnp.bfloat16) for shape in shapes),
        in_specs=[vectors] * 4,
        out_specs=(anywhere,) * 4,
        scratch_shapes=[pltpu.SemaphoreType.DMA((4,))],
        compiler_params=pltpu.CompilerParams(vmem_limit_bytes=2**20),
    )(*mixed)


def kernel_fits(n, video_rows, audio_rows):
    if n < 4 or n % 2 or HV % n or HA % n or (HV // n * HDV) % LANES or (HA // n * HDA) % LANES:
        return False
    ratio = video_rows // audio_rows
    return video_rows == ratio * audio_rows and ratio & (ratio - 1) == 0 and n * audio_rows % 16 == 0 and audio_rows % 8 == 0


def dispatch(*arguments):
    fits = kernel_fits(lax.axis_size("seq"), arguments[0].shape[0], arguments[3].shape[0])
    return (fused_shards if fits else shards)(*arguments)


def solution(mesh):
    placed = (
        P(("clip", "seq"), None),
        P(("clip", "seq"), None),
        P(("clip", "seq"), None),
        P(("clip", "seq"), None),
        P(("clip", "seq"), None),
        P(("clip", "seq"), None),
        P(("clip", "seq"), None),
        P(("clip", "seq"), None),
        P(("clip", "seq"), None),
        P(("clip", "seq"), None),
        P(("clip", "seq"), None),
        P(("clip", "seq"), None),
        P("clip"),
        P("clip"),
        P("clip"),
    )
    return jax.shard_map(
        dispatch,
        mesh=mesh,
        in_specs=placed,
        out_specs=(
            P(("clip", "seq"), None),
            P(("clip", "seq"), None),
            P(("clip", "seq"), None),
            P(("clip", "seq"), None),
        ),
        check_vma=False,
    )
```
